32 devices in a mesh: ctx: 32 (over z, y, x, core).
Axes of the slice: x: 2, y: 2, z: 4, core: 2. Of those that a mesh axis runs over, the one named last changes fastest.
Arguments:
- queries: bfloat16 [4096, 2048], P('ctx'), may hold values from -128 to 128
- key_heads: bfloat16 [4096, 512], P('ctx'), may hold values from -8 to 8
- value_heads: bfloat16 [4096, 512], P('ctx'), may hold values from -6 to 6
- out_grad: bfloat16 [4096, 2048], P('ctx'), may hold values from -6 to 6
- segment: int32 [4096], P('ctx'), may hold values from 0 to 7, never falling along the last dimension, each value on 1 to 2048 neighbouring positions
- sink_logits: float32 [32], replicated, may hold values from 0 to 4
Outputs:
- query_grad: bfloat16 [4096, 2048], P('ctx')
- key_grad: bfloat16 [4096, 512], P('ctx')
- value_grad: bfloat16 [4096, 512], P('ctx')
- sink_grad: float32 [32], replicated
The draws below stay inside these ranges and needn't reach their ends.
Inputs may be any that keep to these rules, and one draw needn't show every extreme that they name: `segment`: never falls along the tokens; each document holds 1 to 2048 tokens, one exactly that many.
All inputs are finite; a program needn't handle non-finite values.
Results may differ from the reference program's by a relative error of at most 0.008.
Values may be sent and summed in bfloat16 or wider, within the bound.
A program may use at most 128 MiB of HBM per device.

```python
import math
import jax
import jax.numpy as jnp
import numpy as np
from jax import lax

QUERY_HEADS = 32
KV_HEADS = 8
HEAD_DIM = 64
WINDOW = 1024
TOK_DEV = 128
TOKENS = 4096


def shared_keys(key):
    base = jax.random.normal(jax.random.fold_in(key, 101), (TOKENS, KV_HEADS * HEAD_DIM), jnp.float32)
    base = jnp.clip(base, -5.0, 5.0)
    return base


def draw_key_heads(key, part):
    return shared_keys(key).astype(jnp.bfloat16)


def draw_queries(key, part):
    noise = jax.random.normal(jax.random.fold_in(key, 303), (TOKENS, QUERY_HEADS * HEAD_DIM), jnp.float32)
    noise = jnp.clip(noise, -5.0, 5.0)
    return noise.astype(jnp.bfloat16)


def shard_levels(own_key, shape, pieces, low, high):
    def one(dim, parts):
        steps = jax.random.uniform(jax.random.fold_in(jax.random.fold_in(own_key, 6), dim), (parts,), jnp.float32, low / len(pieces), high / len(pieces))
        return jnp.repeat(jnp.exp(steps), shape[dim] // parts).reshape((-1,) + (1,) * (len(shape) - dim - 1))

    gain = one(*pieces[0])
    for cut in pieces[1:]:
        gain = gain * one(*cut)
    return gain


def profile(number_of, total, bound, lean):
    loads = [(1 << 20) // math.isqrt(rank ** lean) + 1 for rank in range(2, number_of + 1)]
    surplus, counts = total - bound - (number_of - 1), [1] * (number_of - 1)
    while surplus > 0:
        movable = [i for i in range(number_of - 1) if counts[i] < bound]
        mass, remaining = sum([loads[i] for i in movable]), surplus
        for i in movable:
            extra = min(bound - counts[i], max(1, remaining * loads[i] // mass), surplus)
            counts[i] = counts[i] + extra
            surplus = surplus - extra
    return np.array([bound] + counts)


def uneven(stream_key, amount, total, limit, skew):
    if amount == 2:
        one = jax.random.randint(stream_key, (), max(1, total - limit), min(limit, total - 1) + 1)
        return jnp.stack([one, total - one])
    sizes = jnp.asarray(profile(amount, total, limit, skew), jnp.int32)
    pairs = (amount - 1) // 2
    source_of, taker = sizes[1:1 + 2 * pairs:2], sizes[2:2 + 2 * pairs:2]
    slack = jnp.minimum(source_of - 1, limit - taker)
    passed = jax.random.randint(jax.random.fold_in(stream_key, 1), (pairs,), 0, 1 << 20) % (slack + 1)
    sizes = sizes.at[1:1 + 2 * pairs:2].set(source_of - passed).at[2:2 + 2 * pairs:2].set(taker + passed)
    return sizes[jax.random.permutation(jax.random.fold_in(stream_key, 2), amount)]


def gaussian(own_key, shape, width, most, cuts=(), kind=jnp.bfloat16):
    drawn = width * jax.random.normal(own_key, shape, jnp.float32)
    if cuts:
        drawn = drawn * shard_levels(own_key, shape, cuts, -0.22, 0.18)
    return jnp.clip(drawn, -most, most).astype(kind)


def setup_inputs(seed: int = 0) -> dict:
    splits = jax.random.split(jax.random.key(seed), 7)
    queries = draw_queries(jax.random.fold_in(splits[6], 71), 0)
    key_heads = draw_key_heads(jax.random.fold_in(splits[6], 71), 0)
    value_heads = gaussian(splits[2], (TOKENS, KV_HEADS * HEAD_DIM), 1.0, 6.0, ((0, 32),))
    out_grad = gaussian(splits[3], (TOKENS, QUERY_HEADS * HEAD_DIM), 1.0, 6.0, ((0, 32),))
    segment = jnp.searchsorted(jnp.cumsum(uneven(splits[4], TOKENS // (4 * TOK_DEV), TOKENS, 16 * TOK_DEV, 2)), jnp.arange(TOKENS), side="right").astype(jnp.int32)
    sink_logits = jnp.clip(jax.random.uniform(splits[5], (QUERY_HEADS,), jnp.float32, 0.0, 4.0), 0.0, 4.0)
    return dict(queries=queries, key_heads=key_heads, value_heads=value_heads, out_grad=out_grad, segment=segment, sink_logits=sink_logits)


def block_grads(q_block, k_block, v_block, grad_block, allowed, sink_logits):
    groups = QUERY_HEADS // KV_HEADS
    score_scale = 1.0 / math.sqrt(HEAD_DIM)
    query_four = q_block.astype(jnp.float32).reshape(TOK_DEV, KV_HEADS, groups, HEAD_DIM)
    key_three = k_block.astype(jnp.float32).reshape(-1, KV_HEADS, HEAD_DIM)
    value_three = v_block.astype(jnp.float32).reshape(-1, KV_HEADS, HEAD_DIM)
    grad_four = grad_block.astype(jnp.float32).reshape(TOK_DEV, KV_HEADS, groups, HEAD_DIM)
    scores = jnp.einsum('bhgd,lhd->hgbl', query_four, key_three) * score_scale
    scores = jnp.where(allowed, scores, -jnp.inf)
    sink_grid = sink_logits.astype(jnp.float32).reshape(KV_HEADS, groups, 1, 1)
    top_value = jnp.maximum(lax.optimization_barrier(jnp.max(scores, -1, keepdims=True)), sink_grid)
    expd = jnp.exp(scores - top_value)
    sink_exp = jnp.exp(sink_grid - top_value)
    denom = lax.optimization_barrier(jnp.sum(expd, -1, keepdims=True)) + sink_exp
    probs = expd / denom
    sink_prob = (sink_exp / denom)[..., 0]
    weights = lax.optimization_barrier(probs.astype(jnp.bfloat16)).astype(jnp.float32)
    attended = jnp.einsum('hgbl,lhd->hgbd', weights, value_three)
    delta = jnp.einsum('bhgd,hgbd->hgb', grad_four, attended)
    dprob = jnp.einsum('bhgd,lhd->hgbl', grad_four, value_three)
    dscore = probs * (dprob - delta[..., None])
    dscore_b = lax.optimization_barrier(dscore.astype(jnp.bfloat16)).astype(jnp.float32)
    query_part = jnp.einsum('hgbl,lhd->bhgd', dscore_b, key_three) * score_scale
    key_part = jnp.einsum('hgbl,bhgd->lhd', dscore_b, query_four) * score_scale
    value_part = jnp.einsum('hgbl,bhgd->lhd', weights, grad_four)
    sink_part = -lax.optimization_barrier(jnp.sum(sink_prob * delta, -1)).reshape(QUERY_HEADS)
    query_part = query_part.reshape(TOK_DEV, QUERY_HEADS * HEAD_DIM).astype(jnp.bfloat16)
    key_part = key_part.reshape(-1, KV_HEADS * HEAD_DIM)
    value_part = value_part.reshape(-1, KV_HEADS * HEAD_DIM)
    return (query_part, key_part, value_part, sink_part)

def reference(queries, key_heads, value_heads, out_grad, segment, sink_logits):
    key_span = WINDOW + TOK_DEV
    kv_width = KV_HEADS * HEAD_DIM
    key_padded = jnp.concatenate([jnp.zeros((WINDOW, kv_width), key_heads.dtype), key_heads], 0)
    value_padded = jnp.concatenate([jnp.zeros((WINDOW, kv_width), value_heads.dtype), value_heads], 0)
    segment_padded = jnp.concatenate([jnp.full((WINDOW,), -1, jnp.int32), segment.astype(jnp.int32)], 0)
    query_pos = jnp.arange(TOK_DEV, dtype=jnp.int32)[:, None]
    key_pos = jnp.arange(key_span, dtype=jnp.int32)[None, :]
    inside = (key_pos > query_pos) & (key_pos <= query_pos + WINDOW)

    def one_block(running, block_index):
        key_acc, value_acc, sink_acc = running
        offset = (block_index * TOK_DEV).astype(jnp.int32)
        q_block = lax.dynamic_slice_in_dim(queries, offset, TOK_DEV, 0)
        grad_block = lax.dynamic_slice_in_dim(out_grad, offset, TOK_DEV, 0)
        k_block = lax.dynamic_slice_in_dim(key_padded, offset, key_span, 0)
        v_block = lax.dynamic_slice_in_dim(value_padded, offset, key_span, 0)
        seg_query = lax.dynamic_slice_in_dim(segment.astype(jnp.int32), offset, TOK_DEV, 0)
        seg_key = lax.dynamic_slice_in_dim(segment_padded, offset, key_span, 0)
        allowed = inside & (seg_query[:, None] == seg_key[None, :])
        query_part, key_part, value_part, sink_part = block_grads(q_block, k_block, v_block, grad_block, allowed, sink_logits)
        key_acc = lax.dynamic_update_slice_in_dim(key_acc, lax.dynamic_slice_in_dim(key_acc, offset, key_span, 0) + key_part, offset, 0)
        value_acc = lax.dynamic_update_slice_in_dim(value_acc, lax.dynamic_slice_in_dim(value_acc, offset, key_span, 0) + value_part, offset, 0)
        return ((key_acc, value_acc, sink_acc + sink_part), query_part)
    initial = (jnp.zeros((WINDOW + TOKENS, kv_width), jnp.float32), jnp.zeros((WINDOW + TOKENS, kv_width), jnp.float32), jnp.zeros((QUERY_HEADS,), jnp.float32))
    indices = jnp.arange(TOKENS // TOK_DEV, dtype=jnp.int32)
    (key_acc, value_acc, sink_acc), query_blocks = lax.scan(one_block, initial, indices)
    query_grad = query_blocks.reshape(TOKENS, QUERY_HEADS * HEAD_DIM)
    return (query_grad, key_acc[WINDOW:].astype(jnp.bfloat16), value_acc[WINDOW:].astype(jnp.bfloat16), sink_acc)
```

```python
import functools

import jax
import jax.numpy as jnp
from jax import lax
from jax.experimental import pallas as pl
from jax.experimental.pallas import tpu as pltpu
from jax.sharding import PartitionSpec as P

QUERY_HEADS = 32
KV_HEADS = 8
HEAD_DIM = 64
WINDOW = 1024
GROUPS = QUERY_HEADS // KV_HEADS
MESH = pl.DeviceIdType.MESH
F32 = jnp.float32
BF16 = jnp.bfloat16
MASKED = -1e30


def flip(index, mask):
    result = index
    for bit in (1, 2, 4):
        on = (mask // bit) % 2
        result = result + on * (bit - 2 * bit * ((index // bit) % 2))
    return result


def kernel(planes, chunk, sink_ref, q_ref, k_ref, v_ref, g_ref, seg_ref, oq_ref, ok_ref, ov_ref, os_ref,
           kvsend, segsend, kvbuf, segbuf, qbuf, gbuf, ktbuf, segcol, rhs, grhs, sd, ed, acc,
           qgs, kvgs, kvin, kvnx, sinkacc, sinkplanes, sinksum, sinkall,
           s_kv, r_kv, s_seg, r_seg, s_q, r_q, s_g, r_g, s_qg, r_qg, s_kg, r_kg, s_sa, r_sa, s_sb, r_sb):
    tok = q_ref.shape[0]
    side = KV_HEADS
    cols = GROUPS * HEAD_DIM
    lanes = GROUPS * tok
    span = WINDOW + tok
    me = lax.axis_index("ctx")
    l = me % side
    z = me // side
    base = z * side

    def rows(j):
        return pl.ds(pl.multiple_of(j * tok, tok), tok)

    def head_cols(d):
        return pl.ds(pl.multiple_of(d * cols, cols), cols)

    def remote(src, dst, ssem, rsem, device):
        return pltpu.make_async_remote_copy(
            src_ref=src, dst_ref=dst, send_sem=ssem, recv_sem=rsem,
            device_id=(device,), device_id_type=MESH)

    barrier = pltpu.get_barrier_semaphore()

    def greet(device):
        pl.semaphore_signal(barrier, inc=1, device_id=(device,), device_id_type=MESH)

    for k in range(1, side):
        greet(base + flip(l, k))

    @pl.when(z > 0)
    def _():
        for k in range(side):
            greet(base - side + k)

    @pl.when(z < planes - 1)
    def _():
        for k in range(side):
            greet(base + side + k)

    for p in range(planes):
        @pl.when((p > z + 1) | (p < z - 1))
        def _():
            greet(p * side + l)

    for h in range(side):
        part = slice(h * HEAD_DIM, (h + 1) * HEAD_DIM)
        kvsend[h] = jnp.concatenate([k_ref[:, part], v_ref[:, part]], 1)
    segsend[...] = jnp.broadcast_to(seg_ref[...].astype(F32), segsend.shape)
    kvbuf[rows(side + l), :] = kvsend[l]
    segbuf[side + l] = segsend[...]
    qbuf[l] = q_ref[:, head_cols(l)]
    gbuf[l] = g_ref[:, head_cols(l)]
    acc[...] = jnp.zeros_like(acc)
    sinkacc[...] = jnp.zeros_like(sinkacc)

    @pl.when(z == 0)
    def _():
        kvbuf[0:WINDOW, :] = jnp.zeros((WINDOW, kvbuf.shape[1]), BF16)
        segbuf[0:side] = jnp.full((side,) + segbuf.shape[1:], -1.0, F32)

    @pl.when(z == planes - 1)
    def _():
        kvnx[...] = jnp.zeros_like(kvnx)

    ends = (z + planes - 1) // planes + (2 * planes - 2 - z) // planes
    pl.semaphore_wait(barrier, side - 1 + planes - 1 + (side - 1) * ends)

    def kv_next(k):
        d = flip(l, k)
        return (remote(kvsend.at[d], kvbuf.at[rows(l)], s_kv.at[k], r_kv.at[l], base + side + d),
                remote(segsend, segbuf.at[l], s_seg.at[k], r_seg.at[l], base + side + d))

    def kv_own(k):
        d = flip(l, k)
        return (remote(kvsend.at[d], kvbuf.at[rows(side + l)], s_kv.at[side + k], r_kv.at[side + l], base + d),
                remote(segsend, segbuf.at[side + l], s_seg.at[side + k], r_seg.at[side + l], base + d))

    def qg_to(k):
        d = flip(l, k)
        return (remote(q_ref.at[:, head_cols(d)], qbuf.at[l], s_q.at[k], r_q.at[l], base + d),
                remote(g_ref.at[:, head_cols(d)], gbuf.at[l], s_g.at[k], r_g.at[l], base + d))

    @pl.when(z < planes - 1)
    def _():
        for k in range(side):
            for copy in kv_next(k):
                copy.start()

    for k in range(1, side):
        for copy in kv_own(k):
            copy.start()
    for k in range(1, side):
        for copy in qg_to(k):
            copy.start()

    other = base + flip(l, 1)

    def kv_arrive(j):
        remote(kvsend.at[0], kvbuf.at[rows(j)], s_kv.at[0], r_kv.at[j], other).wait_recv()
        remote(segsend, segbuf.at[j], s_seg.at[0], r_seg.at[j], other).wait_recv()

    for k in range(1, side):
        kv_arrive(side + flip(l, k))

    @pl.when(z > 0)
    def _():
        for k in range(side):
            kv_arrive(k)

    for j in range(2 * side):
        block = kvbuf[j * tok:(j + 1) * tok, :].astype(F32)
        ktbuf[:, j * tok:(j + 1) * tok] = block.T[:HEAD_DIM].astype(BF16)
        segcol[j * tok:(j + 1) * tok, :] = jnp.broadcast_to(segbuf[j, 0:1], (tok, tok)).T

    sink_row = jnp.concatenate(
        [jnp.full((1, tok), sink_ref[GROUPS * l + h], F32) for h in range(GROUPS)], 1)
    zero = jnp.zeros((tok, HEAD_DIM), BF16)

    def qg_back(k):
        b = flip(l, k)
        return remote(qgs.at[b], oq_ref.at[:, head_cols(l)], s_qg.at[b], r_qg.at[l], base + b)

    def step(k, carry):
        b = flip(l, k)

        @pl.when(k > 0)
        def _():
            remote(q_ref.at[:, head_cols(0)], qbuf.at[b], s_q.at[0], r_q.at[b], other).wait_recv()
            remote(g_ref.at[:, head_cols(0)], gbuf.at[b], s_g.at[0], r_g.at[b], other).wait_recv()

        q = (qbuf[b].astype(F32) * 0.125).astype(BF16)
        g = gbuf[b]
        for h in range(GROUPS):
            part = slice(h * HEAD_DIM, (h + 1) * HEAD_DIM)
            rhs[h * tok:(h + 1) * tok, :] = jnp.concatenate([q[:, part], zero], 1)
            rhs[lanes + h * tok:lanes + (h + 1) * tok, :] = jnp.concatenate([zero, g[:, part]], 1)

        seg_row = segbuf[side + b, 0:1, :]
        start = pl.multiple_of(b * tok, tok)
        lane = lax.broadcasted_iota(jnp.int32, (chunk, tok), 1)
        sub = lax.broadcasted_iota(jnp.int32, (chunk, tok), 0)

        def scores(c, top):
            first = pl.multiple_of(c * chunk, chunk)
            both = lax.dot_general(kvbuf[pl.ds(start + first, chunk), :], rhs[...],
                                   (((1,), (1,)), ((), ())), preferred_element_type=F32)
            rel = sub + first - lane
            keep = (rel > 0) & (rel <= WINDOW) & (segcol[pl.ds(start + first, chunk), :] == seg_row)
            tops = []
            for h in range(GROUPS):
                part = jnp.where(keep, both[:, h * tok:(h + 1) * tok], MASKED)
                sd[pl.ds(first, chunk), h * tok:(h + 1) * tok] = part
                tops.append(jnp.max(part.reshape(chunk // 8, 8, tok), 0))
            sd[pl.ds(first, chunk), lanes:] = both[:, lanes:]
            return jnp.maximum(top, jnp.concatenate(tops, 1))

        top = lax.fori_loop(0, span // chunk, scores, jnp.broadcast_to(sink_row, (8, lanes)))
        top = jnp.max(top, 0, keepdims=True)

        small = chunk // 3

        def expd(c, carry):
            total, mixed = carry
            first = pl.multiple_of(c * small, small)
            e = jnp.exp(sd[pl.ds(first, small), :lanes] - top)
            dp = sd[pl.ds(first, small), lanes:]
            sd[pl.ds(first, small), :lanes] = e
            ed[pl.ds(first, small), lanes:] = e.astype(BF16)
            total = total + jnp.sum(e.reshape(small // 8, 8, lanes), 0)
            mixed = mixed + jnp.sum((e * dp).reshape(small // 8, 8, lanes), 0)
            return total, mixed

        empty = jnp.zeros((8, lanes), F32)
        total, mixed = lax.fori_loop(0, span // small, expd, (empty, empty))
        sink_exp = jnp.exp(sink_row - top)
        inv = 1.0 / (jnp.sum(total, 0, keepdims=True) + sink_exp)
        delta = jnp.sum(mixed, 0, keepdims=True) * inv
        sinkacc[...] = sinkacc[...] - jnp.broadcast_to(sink_exp * inv * delta, sinkacc.shape)

        for h in range(GROUPS):
            inv_col = jnp.broadcast_to(inv[:, h * tok:(h + 1) * tok], (tok, tok)).T
            for r in (h * tok, lanes + h * tok):
                grhs[r:r + tok, :] = (rhs[r:r + tok, :].astype(F32) * inv_col).astype(BF16)

        def grads(c, qgt):
            first = pl.multiple_of(c * chunk, chunk)
            d = (sd[pl.ds(first, chunk), :lanes] * (sd[pl.ds(first, chunk), lanes:] - delta)).astype(BF16)
            ed[pl.ds(first, chunk), :lanes] = d
            acc[pl.ds(start + first, chunk), :] += jnp.dot(
                ed[pl.ds(first, chunk), :], grhs[...], preferred_element_type=F32)
            return qgt + jnp.dot(ktbuf[:, pl.ds(pl.multiple_of(start + first, tok), chunk)], d,
                                 preferred_element_type=F32)

        qgt = lax.fori_loop(0, span // chunk, grads, jnp.zeros((HEAD_DIM, lanes), F32))
        qgt = qgt * (inv * 0.125)
        for pair in range(GROUPS // 2):
            two = jnp.concatenate(
                [qgt[:, (2 * pair + i) * tok:(2 * pair + i + 1) * tok] for i in (0, 1)], 0)
            qgs[b, :, pair * tok:(pair + 1) * tok] = two.T.astype(BF16)

        @pl.when(k > 0)
        def _():
            qg_back(k).start()
        return carry

    lax.fori_loop(0, side, step, 0)

    for j in range(2 * side):
        kvgs[j] = acc[j * tok:(j + 1) * tok, :].astype(BF16)
    for h in range(GROUPS):
        sinksum[h:h + 1, :] = sinkacc[0:1, h * tok:(h + 1) * tok]
    sinksum[GROUPS:, :] = jnp.zeros((8 - GROUPS, tok), F32)
    oq_ref[:, head_cols(l)] = qgs[l]
    kvin[l] = kvgs[side + l]
    sinkplanes[z] = sinksum[...]

    def kg_prev(k):
        d = flip(l, k)
        return remote(kvgs.at[d], kvnx.at[l], s_kg.at[k], r_kg.at[l], base - side + d)

    def kg_own(k):
        d = flip(l, k)
        return remote(kvgs.at[side + d], kvin.at[l], s_kg.at[side + k], r_kg.at[side + l], base + d)

    def sink_to(p):
        return remote(sinksum, sinkplanes.at[z], s_sa.at[p], r_sa.at[z], p * side + l)

    @pl.when(z > 0)
    def _():
        for k in range(side):
            kg_prev(k).start()

    for p in range(planes):
        @pl.when(p != z)
        def _():
            sink_to(p).start()

    for k in range(1, side):
        kg_own(k).start()

    for p in range(planes):
        @pl.when(p != z)
        def _():
            remote(sinksum, sinkplanes.at[p], s_sa.at[p], r_sa.at[p], other).wait_recv()

    sinkall[l] = jnp.sum(sinkplanes[...], 0)

    def sink_side(k):
        return remote(sinkall.at[l], sinkall.at[l], s_sb.at[k], r_sb.at[l], base + flip(l, k))

    for k in range(1, side):
        sink_side(k).start()

    for k in range(1, side):
        j = flip(l, k)
        remote(kvgs.at[0], kvin.at[j], s_kg.at[0], r_kg.at[side + j], other).wait_recv()

    @pl.when(z < planes - 1)
    def _():
        for k in range(side):
            remote(kvgs.at[0], kvnx.at[k], s_kg.at[0], r_kg.at[k], other).wait_recv()

    for pair in range(side // 2):
        two = [kvin[2 * pair + i].astype(F32) + kvnx[2 * pair + i].astype(F32) for i in (0, 1)]
        part = slice(pair * 2 * HEAD_DIM, (pair + 1) * 2 * HEAD_DIM)
        ok_ref[:, part] = jnp.concatenate([t[:, :HEAD_DIM] for t in two], 1).astype(BF16)
        ov_ref[:, part] = jnp.concatenate([t[:, HEAD_DIM:] for t in two], 1).astype(BF16)

    for k in range(1, side):
        j = flip(l, k)
        remote(sinkall.at[j], sinkall.at[j], s_sb.at[0], r_sb.at[j], other).wait_recv()
    os_ref[...] = jnp.sum(sinkall[...], -1)

    for k in range(1, side):
        j = flip(l, k)
        remote(qgs.at[0], oq_ref.at[:, head_cols(j)], s_qg.at[0], r_qg.at[j], other).wait_recv()

    @pl.when(z < planes - 1)
    def _():
        for k in range(side):
            for copy in kv_next(k):
                copy.wait_send()

    @pl.when(z > 0)
    def _():
        for k in range(side):
            kg_prev(k).wait_send()

    for p in range(planes):
        @pl.when(p != z)
        def _():
            sink_to(p).wait_send()

    for k in range(1, side):
        for copy in kv_own(k) + qg_to(k) + (qg_back(k), kg_own(k), sink_side(k)):
            copy.wait_send()


def per_device(queries, key_heads, value_heads, out_grad, segment, sink_logits):
    tok = queries.shape[0]
    planes = lax.axis_size("ctx") // KV_HEADS
    side = KV_HEADS
    cols = GROUPS * HEAD_DIM
    lanes = GROUPS * tok
    span = WINDOW + tok
    chunk = span // 3
    wide = 2 * HEAD_DIM
    vmem = pl.BlockSpec(memory_space=pltpu.VMEM)
    dma = pltpu.SemaphoreType.DMA
    scratch = [
        pltpu.VMEM((side, tok, wide), BF16),
        pltpu.VMEM((8, tok), F32),
        pltpu.VMEM((2 * WINDOW, wide), BF16),
        pltpu.VMEM((2 * side, 8, tok), F32),
        pltpu.VMEM((side, tok, cols), BF16),
        pltpu.VMEM((side, tok, cols), BF16),
        pltpu.VMEM((HEAD_DIM, 2 * WINDOW), BF16),
        pltpu.VMEM((2 * WINDOW, tok), F32),
        pltpu.VMEM((2 * lanes, wide), BF16),
        pltpu.VMEM((2 * lanes, wide), BF16),
        pltpu.VMEM((span, 2 * lanes), F32),
        pltpu.VMEM((span, 2 * lanes), BF16),
        pltpu.VMEM((2 * WINDOW, wide), F32),
        pltpu.VMEM((side, tok, cols), BF16),
        pltpu.VMEM((2 * side, tok, wide), BF16),
        pltpu.VMEM((side, tok, wide), BF16),
        pltpu.VMEM((side, tok, wide), BF16),
        pltpu.VMEM((8, lanes), F32),
        pltpu.VMEM((planes, 8, tok), F32),
        pltpu.VMEM((8, tok), F32),
        pltpu.VMEM((side, 8, tok), F32),
        dma((2 * side,)), dma((2 * side,)), dma((2 * side,)), dma((2 * side,)),
        dma((side,)), dma((side,)), dma((side,)), dma((side,)),
        dma((side,)), dma((side,)), dma((2 * side,)), dma((2 * side,)),
        dma((planes,)), dma((planes,)), dma((side,)), dma((side,)),
    ]
    query_grad, key_grad, value_grad, sink = pl.pallas_call(
        functools.partial(kernel, planes, chunk),
        out_shape=(
            jax.ShapeDtypeStruct(queries.shape, BF16),
            jax.ShapeDtypeStruct(key_heads.shape, BF16),
            jax.ShapeDtypeStruct(value_heads.shape, BF16),
            jax.ShapeDtypeStruct((side, 8), F32),
        ),
        in_specs=[pl.BlockSpec(memory_space=pltpu.SMEM)] + [vmem] * 5,
        out_specs=(vmem,) * 4,
        scratch_shapes=scratch,
        compiler_params=pltpu.CompilerParams(
            collective_id=0, has_side_effects=True, vmem_limit_bytes=48 * 1024 * 1024),
    )(sink_logits, queries, key_heads, value_heads, out_grad, segment.reshape(1, tok))
    return query_grad, key_grad, value_grad, sink[:, :GROUPS].reshape(-1)


def solution(mesh):
    return jax.shard_map(
        per_device,
        mesh=mesh,
        in_specs=(P("ctx", None), P("ctx", None), P("ctx", None), P("ctx", None), P("ctx"), P()),
        out_specs=(P("ctx", None), P("ctx", None), P("ctx", None), P()),
        check_vma=False,
    )
```

```python
import functools

import jax
import jax.numpy as jnp
from jax import lax
from jax.experimental import pallas as pl
from jax.experimental.pallas import tpu as pltpu
from jax.sharding import PartitionSpec as P

QUERY_HEADS = 32
KV_HEADS = 8
HEAD_DIM = 64
WINDOW = 1024
GROUPS = QUERY_HEADS // KV_HEADS
MESH = pl.DeviceIdType.MESH
F32 = jnp.float32
BF16 = jnp.bfloat16
MASKED = -1e30


def flip(index, mask):
    result = index
    for bit in (1, 2, 4):
        on = (mask // bit) % 2
        result = result + on * (bit - 2 * bit * ((index // bit) % 2))
    return result


def kernel(planes, chunk, sink_hbm, q_ref, k_hbm, v_hbm, g_ref, seg_hbm, oq_ref, ok_ref, ov_ref, os_ref,
           sink_ref, k_ref, v_ref, seg_ref, s_in, kvsend, segsend, kvbuf, segbuf, qbuf, gbuf, ktbuf, segcol, rhs, grhs, sd, ed, acc,
           qgs, kvgs, kvin, kvnx, sinkacc, sinkplanes, sinksum, sinkall,
           s_kv, r_kv, s_seg, r_seg, s_q, r_q, s_g, r_g, s_qg, r_qg, s_kg, r_kg, s_sa, r_sa, s_sb, r_sb):
    tok = q_ref.shape[0]
    side = KV_HEADS
    cols = GROUPS * HEAD_DIM
    lanes = GROUPS * tok
    span = WINDOW + tok
    me = lax.axis_index("ctx")
    l = me % side
    z = me // side
    base = z * side

    def rows(j):
        return pl.ds(pl.multiple_of(j * tok, tok), tok)

    def head_cols(d):
        return pl.ds(pl.multiple_of(d * cols, cols), cols)

    def remote(src, dst, ssem, rsem, device):
        return pltpu.make_async_remote_copy(
            src_ref=src, dst_ref=dst, send_sem=ssem, recv_sem=rsem,
            device_id=(device,), device_id_type=MESH)

    inputs = [
        pltpu.make_async_copy(k_hbm, k_ref, s_in.at[0]),
        pltpu.make_async_copy(v_hbm, v_ref, s_in.at[1]),
        pltpu.make_async_copy(seg_hbm, seg_ref, s_in.at[2]),
        pltpu.make_async_copy(sink_hbm, sink_ref, s_in.at[3]),
        pltpu.make_async_copy(q_ref.at[:, head_cols(l)], qbuf.at[l], s_in.at[4]),
        pltpu.make_async_copy(g_ref.at[:, head_cols(l)], gbuf.at[l], s_in.at[5]),
    ]
    for copy in inputs:
        copy.start()

    barrier = pltpu.get_barrier_semaphore()

    def greet(device):
        pl.semaphore_signal(barrier, inc=1, device_id=(device,), device_id_type=MESH)

    for k in range(1, side):
        greet(base + flip(l, k))

    @pl.when(z > 0)
    def _():
        for k in range(side):
            greet(base - side + k)

    @pl.when(z < planes - 1)
    def _():
        for k in range(side):
            greet(base + side + k)

    for p in range(planes):
        @pl.when((p > z + 1) | (p < z - 1))
        def _():
            greet(p * side + l)

    for copy in inputs[:3]:
        copy.wait()
    for h in range(side):
        part = slice(h * HEAD_DIM, (h + 1) * HEAD_DIM)
        kvsend[h] = jnp.concatenate([k_ref[:, part], v_ref[:, part]], 1)
    segsend[...] = jnp.broadcast_to(seg_ref[...].astype(F32), segsend.shape)
    kvbuf[rows(side + l), :] = kvsend[l]
    segbuf[side + l] = segsend[...]
    acc[...] = jnp.zeros_like(acc)
    sinkacc[...] = jnp.zeros_like(sinkacc)

    @pl.when(z == 0)
    def _():
        kvbuf[0:WINDOW, :] = jnp.zeros((WINDOW, kvbuf.shape[1]), BF16)
        segbuf[0:side] = jnp.full((side,) + segbuf.shape[1:], -1.0, F32)

    @pl.when(z == planes - 1)
    def _():
        kvnx[...] = jnp.zeros_like(kvnx)

    ends = (z + planes - 1) // planes + (2 * planes - 2 - z) // planes
    pl.semaphore_wait(barrier, side - 1 + planes - 1 + (side - 1) * ends)

    def kv_next(k):
        d = flip(l, k)
        return (remote(kvsend.at[d], kvbuf.at[rows(l)], s_kv.at[k], r_kv.at[l], base + side + d),
                remote(segsend, segbuf.at[l], s_seg.at[k], r_seg.at[l], base + side + d))

    def kv_own(k):
        d = flip(l, k)
        return (remote(kvsend.at[d], kvbuf.at[rows(side + l)], s_kv.at[side + k], r_kv.at[side + l], base + d),
                remote(segsend, segbuf.at[side + l], s_seg.at[side + k], r_seg.at[side + l], base + d))

    def qg_to(k):
        d = flip(l, k)
        return (remote(q_ref.at[:, head_cols(d)], qbuf.at[l], s_q.at[k], r_q.at[l], base + d),
                remote(g_ref.at[:, head_cols(d)], gbuf.at[l], s_g.at[k], r_g.at[l], base + d))

    @pl.when(z < planes - 1)
    def _():
        for k in range(side):
            for copy in kv_next(k):
                copy.start()

    for k in range(1, side):
        for copy in kv_own(k):
            copy.start()
    for k in range(1, side):
        for copy in qg_to(k):
            copy.start()

    other = base + flip(l, 1)

    def kv_arrive(j):
        remote(kvsend.at[0], kvbuf.at[rows(j)], s_kv.at[0], r_kv.at[j], other).wait_recv()
        remote(segsend, segbuf.at[j], s_seg.at[0], r_seg.at[j], other).wait_recv()

    for k in range(1, side):
        kv_arrive(side + flip(l, k))

    @pl.when(z > 0)
    def _():
        for k in range(side):
            kv_arrive(k)

    for j in range(2 * side):
        block = kvbuf[j * tok:(j + 1) * tok, :].astype(F32)
        ktbuf[:, j * tok:(j + 1) * tok] = block.T[:HEAD_DIM].astype(BF16)
        segcol[j * tok:(j + 1) * tok, :] = jnp.broadcast_to(segbuf[j, 0:1], (tok, tok)).T

    for copy in inputs[3:]:
        copy.wait()
    sink_row = jnp.concatenate(
        [jnp.full((1, tok), sink_ref[GROUPS * l + h], F32) for h in range(GROUPS)], 1)
    zero = jnp.zeros((tok, HEAD_DIM), BF16)

    def qg_back(k):
        b = flip(l, k)
        return remote(qgs.at[b], oq_ref.at[:, head_cols(l)], s_qg.at[b], r_qg.at[l], base + b)

    lane = lax.broadcasted_iota(jnp.int32, (chunk, tok), 1)
    sub = lax.broadcasted_iota(jnp.int32, (chunk, tok), 0)
    floor = jnp.broadcast_to(sink_row, (8, lanes))
    empty = jnp.zeros((8, lanes), F32)

    def prepare(k, slot):
        b = flip(l, k)
        q = (qbuf[b].astype(F32) * 0.125).astype(BF16)
        g = gbuf[b]
        for h in range(GROUPS):
            part = slice(h * HEAD_DIM, (h + 1) * HEAD_DIM)
            rhs[slot, h * tok:(h + 1) * tok, :] = jnp.concatenate([q[:, part], zero], 1)
            rhs[slot, lanes + h * tok:lanes + (h + 1) * tok, :] = jnp.concatenate([zero, g[:, part]], 1)

    def arrive(k):
        b = flip(l, k)
        remote(q_ref.at[:, head_cols(0)], qbuf.at[b], s_q.at[0], r_q.at[b], other).wait_recv()
        remote(g_ref.at[:, head_cols(0)], gbuf.at[b], s_g.at[0], r_g.at[b], other).wait_recv()

    def scores(c, k, slot, top):
        b = flip(l, k)
        seg_row = segbuf[side + b, 0:1, :]
        first = pl.multiple_of(c * chunk, chunk)
        at = pl.ds(pl.multiple_of(b * tok + c * chunk, tok), chunk)
        both = lax.dot_general(kvbuf[at, :], rhs[slot],
                               (((1,), (1,)), ((), ())), preferred_element_type=F32)
        rel = sub + first - lane
        keep = (rel > 0) & (rel <= WINDOW) & (segcol[at, :] == seg_row)
        tops = []
        for h in range(GROUPS):
            part = jnp.where(keep, both[:, h * tok:(h + 1) * tok], MASKED)
            sd[slot, pl.ds(first, chunk), h * tok:(h + 1) * tok] = part
            tops.append(jnp.max(part.reshape(chunk // 8, 8, tok), 0))
        sd[slot, pl.ds(first, chunk), lanes:] = both[:, lanes:]
        return jnp.maximum(top, jnp.concatenate(tops, 1))

    def expd(c, slot, top, total, mixed):
        first = pl.multiple_of(c * chunk, chunk)
        e = jnp.exp(sd[slot, pl.ds(first, chunk), :lanes] - top)
        dp = sd[slot, pl.ds(first, chunk), lanes:]
        sd[slot, pl.ds(first, chunk), :lanes] = e
        ed[pl.ds(first, chunk), lanes:] = e.astype(BF16)
        total = total + jnp.sum(e.reshape(chunk // 8, 8, lanes), 0)
        mixed = mixed + jnp.sum((e * dp).reshape(chunk // 8, 8, lanes), 0)
        return total, mixed

    def step(k, top, last):
        b = flip(l, k)
        slot = k % 2
        start = pl.multiple_of(b * tok, tok)
        top = jnp.max(top, 0, keepdims=True)

        if last:
            ahead = floor
            total, mixed = lax.fori_loop(0, span // chunk, lambda c, t: expd(c, slot, top, *t), (empty, empty))
        else:
            arrive(k + 1)
            prepare(k + 1, 1 - slot)

            def both(c, carry):
                ahead, total, mixed = carry
                ahead = scores(c, k + 1, 1 - slot, ahead)
                return (ahead,) + expd(c, slot, top, total, mixed)

            ahead, total, mixed = lax.fori_loop(0, span // chunk, both, (floor, empty, empty))

        sink_exp = jnp.exp(sink_row - top)
        inv = 1.0 / (jnp.sum(total, 0, keepdims=True) + sink_exp)
        delta = jnp.sum(mixed, 0, keepdims=True) * inv
        sinkacc[...] = sinkacc[...] - jnp.broadcast_to(sink_exp * inv * delta, sinkacc.shape)

        for h in range(GROUPS):
            inv_col = jnp.broadcast_to(inv[:, h * tok:(h + 1) * tok], (tok, tok)).T
            for r in (h * tok, lanes + h * tok):
                grhs[r:r + tok, :] = (rhs[slot, r:r + tok, :].astype(F32) * inv_col).astype(BF16)

        def grads(c, qgt):
            first = pl.multiple_of(c * chunk, chunk)
            d = (sd[slot, pl.ds(first, chunk), :lanes]
                 * (sd[slot, pl.ds(first, chunk), lanes:] - delta)).astype(BF16)
            ed[pl.ds(first, chunk), :lanes] = d
            acc[pl.ds(start + first, chunk), :] += jnp.dot(
                ed[pl.ds(first, chunk), :], grhs[...], preferred_element_type=F32)
            return qgt + jnp.dot(ktbuf[:, pl.ds(pl.multiple_of(start + first, tok), chunk)], d,
                                 preferred_element_type=F32)

        qgt = lax.fori_loop(0, span // chunk, grads, jnp.zeros((HEAD_DIM, lanes), F32))
        qgt = qgt * (inv * 0.125)
        for pair in range(GROUPS // 2):
            two = jnp.concatenate(
                [qgt[:, (2 * pair + i) * tok:(2 * pair + i + 1) * tok] for i in (0, 1)], 0)
            qgs[b, :, pair * tok:(pair + 1) * tok] = two.T.astype(BF16)

        @pl.when(k > 0)
        def _():
            qg_back(k).start()
        return ahead

    prepare(0, 0)
    top = lax.fori_loop(0, span // chunk, lambda c, t: scores(c, 0, 0, t), floor)
    top = lax.fori_loop(0, side - 1, lambda k, t: step(k, t, False), top)
    step(side - 1, top, True)

    for j in range(2 * side):
        kvgs[j] = acc[j * tok:(j + 1) * tok, :].astype(BF16)
    for h in range(GROUPS):
        sinksum[h:h + 1, :] = sinkacc[0:1, h * tok:(h + 1) * tok]
    sinksum[GROUPS:, :] = jnp.zeros((8 - GROUPS, tok), F32)
    oq_ref[:, head_cols(l)] = qgs[l]
    kvin[l] = kvgs[side + l]
    sinkplanes[z] = sinksum[...]

    def kg_prev(k):
        d = flip(l, k)
        return remote(kvgs.at[d], kvnx.at[l], s_kg.at[k], r_kg.at[l], base - side + d)

    def kg_own(k):
        d = flip(l, k)
        return remote(kvgs.at[side + d], kvin.at[l], s_kg.at[side + k], r_kg.at[side + l], base + d)

    def sink_to(p):
        return remote(sinksum, sinkplanes.at[z], s_sa.at[p], r_sa.at[z], p * side + l)

    @pl.when(z > 0)
    def _():
        for k in range(side):
            kg_prev(k).start()

    for p in range(planes):
        @pl.when(p != z)
        def _():
            sink_to(p).start()

    for k in range(1, side):
        kg_own(k).start()

    for p in range(planes):
        @pl.when(p != z)
        def _():
            remote(sinksum, sinkplanes.at[p], s_sa.at[p], r_sa.at[p], other).wait_recv()

    sinkall[l] = jnp.sum(sinkplanes[...], 0)

    def sink_side(k):
        return remote(sinkall.at[l], sinkall.at[l], s_sb.at[k], r_sb.at[l], base + flip(l, k))

    for k in range(1, side):
        sink_side(k).start()

    for k in range(1, side):
        j = flip(l, k)
        remote(kvgs.at[0], kvin.at[j], s_kg.at[0], r_kg.at[side + j], other).wait_recv()

    @pl.when(z < planes - 1)
    def _():
        for k in range(side):
            remote(kvgs.at[0], kvnx.at[k], s_kg.at[0], r_kg.at[k], other).wait_recv()

    for pair in range(side // 2):
        two = [kvin[2 * pair + i].astype(F32) + kvnx[2 * pair + i].astype(F32) for i in (0, 1)]
        part = slice(pair * 2 * HEAD_DIM, (pair + 1) * 2 * HEAD_DIM)
        ok_ref[:, part] = jnp.concatenate([t[:, :HEAD_DIM] for t in two], 1).astype(BF16)
        ov_ref[:, part] = jnp.concatenate([t[:, HEAD_DIM:] for t in two], 1).astype(BF16)

    for k in range(1, side):
        j = flip(l, k)
        remote(sinkall.at[j], sinkall.at[j], s_sb.at[0], r_sb.at[j], other).wait_recv()
    place = lax.broadcasted_iota(jnp.int32, sinkall.shape, 2)
    spot = (lax.broadcasted_iota(jnp.int32, sinkall.shape, 0) * GROUPS
            + lax.broadcasted_iota(jnp.int32, sinkall.shape, 1))
    head = lax.broadcasted_iota(jnp.int32, sinkall.shape, 1)
    sums = jnp.sum(sinkall[...], -1, keepdims=True)
    sums = jnp.sum(jnp.where((place == spot) & (head < GROUPS), sums, 0.0), 0)
    os_ref[...] = jnp.sum(sums, 0, keepdims=True)[:, :QUERY_HEADS]

    for k in range(1, side):
        j = flip(l, k)
        remote(qgs.at[0], oq_ref.at[:, head_cols(j)], s_qg.at[0], r_qg.at[j], other).wait_recv()

    @pl.when(z < planes - 1)
    def _():
        for k in range(side):
            for copy in kv_next(k):
                copy.wait_send()

    @pl.when(z > 0)
    def _():
        for k in range(side):
            kg_prev(k).wait_send()

    for p in range(planes):
        @pl.when(p != z)
        def _():
            sink_to(p).wait_send()

    for k in range(1, side):
        for copy in kv_own(k) + qg_to(k) + (qg_back(k), kg_own(k), sink_side(k)):
            copy.wait_send()


def write_out(*refs):
    copies = [pltpu.make_async_copy(refs[i], refs[4 + i], refs[8].at[i]) for i in range(4)]
    for copy in copies:
        copy.start()
    for copy in copies:
        copy.wait()


def per_device(queries, key_heads, value_heads, out_grad, segment, sink_logits):
    tok = queries.shape[0]
    planes = lax.axis_size("ctx") // KV_HEADS
    side = KV_HEADS
    cols = GROUPS * HEAD_DIM
    lanes = GROUPS * tok
    span = WINDOW + tok
    chunk = span // 3
    wide = 2 * HEAD_DIM
    vmem = pl.BlockSpec(memory_space=pltpu.VMEM)
    dma = pltpu.SemaphoreType.DMA
    hbm = pl.BlockSpec(memory_space=pltpu.HBM)
    scratch = [
        pltpu.SMEM((QUERY_HEADS,), F32),
        pltpu.VMEM(key_heads.shape, BF16),
        pltpu.VMEM(key_heads.shape, BF16),
        pltpu.VMEM((1, tok), jnp.int32),
        dma((6,)),
        pltpu.VMEM((side, tok, wide), BF16),
        pltpu.VMEM((8, tok), F32),
        pltpu.VMEM((2 * WINDOW, wide), BF16),
        pltpu.VMEM((2 * side, 8, tok), F32),
        pltpu.VMEM((side, tok, cols), BF16),
        pltpu.VMEM((side, tok, cols), BF16),
        pltpu.VMEM((HEAD_DIM, 2 * WINDOW), BF16),
        pltpu.VMEM((2 * WINDOW, tok), F32),
        pltpu.VMEM((2, 2 * lanes, wide), BF16),
        pltpu.VMEM((2 * lanes, wide), BF16),
        pltpu.VMEM((2, span, 2 * lanes), F32),
        pltpu.VMEM((span, 2 * lanes), BF16),
        pltpu.VMEM((2 * WINDOW, wide), F32),
        pltpu.VMEM((side, tok, cols), BF16),
        pltpu.VMEM((2 * side, tok, wide), BF16),
        pltpu.VMEM((side, tok, wide), BF16),
        pltpu.VMEM((side, tok, wide), BF16),
        pltpu.VMEM((8, lanes), F32),
        pltpu.VMEM((planes, 8, tok), F32),
        pltpu.VMEM((8, tok), F32),
        pltpu.VMEM((side, 8, tok), F32),
        dma((2 * side,)), dma((2 * side,)), dma((2 * side,)), dma((2 * side,)),
        dma((side,)), dma((side,)), dma((side,)), dma((side,)),
        dma((side,)), dma((side,)), dma((2 * side,)), dma((2 * side,)),
        dma((planes,)), dma((planes,)), dma((side,)), dma((side,)),
    ]
    shapes = (
        jax.ShapeDtypeStruct(queries.shape, BF16),
        jax.ShapeDtypeStruct(key_heads.shape, BF16),
        jax.ShapeDtypeStruct(value_heads.shape, BF16),
        jax.ShapeDtypeStruct((1, QUERY_HEADS), F32),
    )
    results = pl.pallas_call(
        functools.partial(kernel, planes, chunk),
        out_shape=shapes,
        in_specs=[hbm] * 6,
        out_specs=(vmem,) * 4,
        scratch_shapes=scratch,
        compiler_params=pltpu.CompilerParams(
            collective_id=0, has_side_effects=True, vmem_limit_bytes=48 * 1024 * 1024),
    )(*[pltpu.with_memory_space_constraint(a, pltpu.HBM) for a in (sink_logits, queries, key_heads, value_heads, out_grad, segment.reshape(1, tok))])
    query_grad, key_grad, value_grad, sink = pl.pallas_call(
        write_out,
        out_shape=shapes,
        in_specs=[vmem] * 4,
        out_specs=(hbm,) * 4,
        scratch_shapes=[dma((4,))],
        compiler_params=pltpu.CompilerParams(vmem_limit_bytes=1024 * 1024),
    )(*results)
    return query_grad, key_grad, value_grad, sink.reshape(-1)


def solution(mesh):
    return jax.shard_map(
        per_device,
        mesh=mesh,
        in_specs=(P("ctx", None), P("ctx", None), P("ctx", None), P("ctx", None), P("ctx"), P()),
        out_specs=(P("ctx", None), P("ctx", None), P("ctx", None), P()),
        check_vma=False,
    )
```

```python
import functools

import jax
import jax.numpy as jnp
from jax import lax
from jax.experimental import pallas as pl
from jax.experimental.pallas import tpu as pltpu
from jax.sharding import PartitionSpec as P

QUERY_HEADS = 32
KV_HEADS = 8
HEAD_DIM = 64
WINDOW = 1024
GROUPS = QUERY_HEADS // KV_HEADS
MESH = pl.DeviceIdType.MESH
F32 = jnp.float32
BF16 = jnp.bfloat16
MASKED = -1e30


def flip(index, mask):
    result = index
    for bit in (1, 2, 4):
        on = (mask // bit) % 2
        result = result + on * (bit - 2 * bit * ((index // bit) % 2))
    return result


def kernel(planes, chunk, sink_hbm, q_ref, k_hbm, v_hbm, g_ref, seg_hbm, oq_ref, ok_ref, ov_ref, os_ref,
           sink_ref, k_ref, v_ref, seg_ref, s_in, kvsend, segsend, kvbuf, segbuf, qbuf, gbuf, ktbuf, segcol, rhs, grhs, sd, ed, acc,
           qgs, kvgs, kvin, kvnx, sinkacc, sinkplanes, sinksum, sinkall,
           s_kv, r_kv, s_seg, r_seg, s_q, r_q, s_g, r_g, s_qg, r_qg, s_kg, r_kg, s_sa, r_sa, s_sb, r_sb):
    tok = q_ref.shape[0]
    side = KV_HEADS
    cols = GROUPS * HEAD_DIM
    lanes = GROUPS * tok
    span = WINDOW + tok
    me = lax.axis_index("ctx")
    l = me % side
    z = me // side
    base = z * side

    def rows(j):
        return pl.ds(pl.multiple_of(j * tok, tok), tok)

    def head_cols(d):
        return pl.ds(pl.multiple_of(d * cols, cols), cols)

    def remote(src, dst, ssem, rsem, device):
        return pltpu.make_async_remote_copy(
            src_ref=src, dst_ref=dst, send_sem=ssem, recv_sem=rsem,
            device_id=(device,), device_id_type=MESH)

    inputs = [
        pltpu.make_async_copy(k_hbm, k_ref, s_in.at[0]),
        pltpu.make_async_copy(v_hbm, v_ref, s_in.at[1]),
        pltpu.make_async_copy(seg_hbm, seg_ref, s_in.at[2]),
        pltpu.make_async_copy(sink_hbm, sink_ref, s_in.at[3]),
        pltpu.make_async_copy(q_ref.at[:, head_cols(l)], qbuf.at[l], s_in.at[4]),
        pltpu.make_async_copy(g_ref.at[:, head_cols(l)], gbuf.at[l], s_in.at[5]),
    ]
    for copy in inputs:
        copy.start()

    barrier = pltpu.get_barrier_semaphore()

    def greet(device):
        pl.semaphore_signal(barrier, inc=1, device_id=(device,), device_id_type=MESH)

    for k in range(1, side):
        greet(base + flip(l, k))

    @pl.when(z > 0)
    def _():
        for k in range(side):
            greet(base - side + k)

    @pl.when(z < planes - 1)
    def _():
        for k in range(side):
            greet(base + side + k)

    for p in range(planes):
        @pl.when((p > z + 1) | (p < z - 1))
        def _():
            greet(p * side + l)

    for copy in inputs[:3]:
        copy.wait()
    for h in range(side):
        part = slice(h * HEAD_DIM, (h + 1) * HEAD_DIM)
        kvsend[h] = jnp.concatenate([k_ref[:, part], v_ref[:, part]], 1)
    segsend[...] = jnp.broadcast_to(seg_ref[...].astype(F32), segsend.shape)
    kvbuf[rows(side + l), :] = kvsend[l]
    segbuf[side + l] = segsend[...]
    acc[...] = jnp.zeros_like(acc)
    sinkacc[...] = jnp.zeros_like(sinkacc)

    @pl.when(z == 0)
    def _():
        kvbuf[0:WINDOW, :] = jnp.zeros((WINDOW, kvbuf.shape[1]), BF16)
        segbuf[0:side] = jnp.full((side,) + segbuf.shape[1:], -1.0, F32)

    @pl.when(z == planes - 1)
    def _():
        kvnx[...] = jnp.zeros_like(kvnx)

    ends = (z + planes - 1) // planes + (2 * planes - 2 - z) // planes
    pl.semaphore_wait(barrier, side - 1 + planes - 1 + (side - 1) * ends)

    def kv_next(k):
        d = flip(l, k)
        return (remote(kvsend.at[d], kvbuf.at[rows(l)], s_kv.at[k], r_kv.at[l], base + side + d),
                remote(segsend, segbuf.at[l], s_seg.at[k], r_seg.at[l], base + side + d))

    def kv_own(k):
        d = flip(l, k)
        return (remote(kvsend.at[d], kvbuf.at[rows(side + l)], s_kv.at[side + k], r_kv.at[side + l], base + d),
                remote(segsend, segbuf.at[side + l], s_seg.at[side + k], r_seg.at[side + l], base + d))

    def qg_to(k):
        d = flip(l, k)
        return (remote(q_ref.at[:, head_cols(d)], qbuf.at[l], s_q.at[k], r_q.at[l], base + d),
                remote(g_ref.at[:, head_cols(d)], gbuf.at[l], s_g.at[k], r_g.at[l], base + d))

    @pl.when(z < planes - 1)
    def _():
        for k in range(side):
            for copy in kv_next(k):
                copy.start()

    for k in range(1, side):
        for copy in kv_own(k):
            copy.start()
    for k in range(1, side):
        for copy in qg_to(k):
            copy.start()

    other = base + flip(l, 1)

    def kv_arrive(j):
        remote(kvsend.at[0], kvbuf.at[rows(j)], s_kv.at[0], r_kv.at[j], other).wait_recv()
        remote(segsend, segbuf.at[j], s_seg.at[0], r_seg.at[j], other).wait_recv()

    def turn_over(j):
        ktbuf[:, rows(j)] = kvbuf[rows(j), :].astype(F32).T[:HEAD_DIM].astype(BF16)
        segcol[rows(j), :] = jnp.broadcast_to(segbuf[j, 0:1], (tok, tok)).T

    for k in range(side):
        if k:
            kv_arrive(side + flip(l, k))
        turn_over(side + flip(l, k))
    for k in range(side):
        @pl.when(z > 0)
        def _():
            kv_arrive(flip(l, k))
        turn_over(flip(l, k))

    for copy in inputs[3:]:
        copy.wait()
    sink_row = jnp.concatenate(
        [jnp.full((1, tok), sink_ref[GROUPS * l + h], F32) for h in range(GROUPS)], 1)
    zero = jnp.zeros((tok, HEAD_DIM), BF16)

    def qg_back(k):
        b = turn(l, k, side)
        return remote(qgs.at[b], oq_ref.at[:, head_cols(l)], s_qg.at[b], r_qg.at[l], base + b)

    lane = lax.broadcasted_iota(jnp.int32, (chunk, tok), 1)
    sub = lax.broadcasted_iota(jnp.int32, (chunk, tok), 0)
    floor = jnp.broadcast_to(sink_row, (8, lanes))
    empty = jnp.zeros((8, lanes), F32)

    def prepare(k, slot):
        b = turn(l, k, side)
        q = (qbuf[b].astype(F32) * 0.125).astype(BF16)
        g = gbuf[b]
        for h in range(GROUPS):
            part = slice(h * HEAD_DIM, (h + 1) * HEAD_DIM)
            rhs[slot, h * tok:(h + 1) * tok, :] = jnp.concatenate([q[:, part], zero], 1)
            rhs[slot, lanes + h * tok:lanes + (h + 1) * tok, :] = jnp.concatenate([zero, g[:, part]], 1)

    def arrive(k):
        b = turn(l, k, side)
        remote(q_ref.at[:, head_cols(0)], qbuf.at[b], s_q.at[0], r_q.at[b], other).wait_recv()
        remote(g_ref.at[:, head_cols(0)], gbuf.at[b], s_g.at[0], r_g.at[b], other).wait_recv()

    def scores(c, k, slot, top):
        b = turn(l, k, side)
        seg_row = segbuf[side + b, 0:1, :]
        first = pl.multiple_of(c * chunk, chunk)
        at = pl.ds(pl.multiple_of(b * tok + c * chunk, tok), chunk)
        both = lax.dot_general(kvbuf[at, :], rhs[slot],
                               (((1,), (1,)), ((), ())), preferred_element_type=F32)
        rel = sub + first - lane
        keep = (rel > 0) & (rel <= WINDOW) & (segcol[at, :] == seg_row)
        tops = []
        for h in range(GROUPS):
            part = jnp.where(keep, both[:, h * tok:(h + 1) * tok], MASKED)
            sd[slot, pl.ds(first, chunk), h * tok:(h + 1) * tok] = part
            tops.append(jnp.max(part.reshape(chunk // 8, 8, tok), 0))
        sd[slot, pl.ds(first, chunk), lanes:] = both[:, lanes:]
        return jnp.maximum(top, jnp.concatenate(tops, 1))

    def expd(c, slot, top, total, mixed):
        first = pl.multiple_of(c * chunk, chunk)
        e = jnp.exp(sd[slot, pl.ds(first, chunk), :lanes] - top)
        dp = sd[slot, pl.ds(first, chunk), lanes:]
        sd[slot, pl.ds(first, chunk), :lanes] = e
        ed[pl.ds(first, chunk), lanes:] = e.astype(BF16)
        total = total + jnp.sum(e.reshape(chunk // 8, 8, lanes), 0)
        mixed = mixed + jnp.sum((e * dp).reshape(chunk // 8, 8, lanes), 0)
        return total, mixed

    def kg_prev(k):
        d = turn(l, k, side)
        return remote(kvgs.at[d], kvnx.at[l], s_kg.at[k], r_kg.at[l], base - side + d)

    def sink_to(p):
        return remote(sinksum, sinkplanes.at[z], s_sa.at[p], r_sa.at[z], p * side + l)

    def step(k, top, last):
        b = turn(l, k, side)
        slot = k % 2
        start = pl.multiple_of(b * tok, tok)
        top = jnp.max(top, 0, keepdims=True)

        if last:
            ahead = floor
            total, mixed = lax.fori_loop(0, span // chunk, lambda c, t: expd(c, slot, top, *t), (empty, empty))
        else:
            arrive(k + 1)
            prepare(k + 1, 1 - slot)

            def both(c, carry):
                ahead, total, mixed = carry
                ahead = scores(c, k + 1, 1 - slot, ahead)
                return (ahead,) + expd(c, slot, top, total, mixed)

            ahead, total, mixed = lax.fori_loop(0, span // chunk, both, (floor, empty, empty))

        sink_exp = jnp.exp(sink_row - top)
        inv = 1.0 / (jnp.sum(total, 0, keepdims=True) + sink_exp)
        delta = jnp.sum(mixed, 0, keepdims=True) * inv
        sinkacc[...] = sinkacc[...] - jnp.broadcast_to(sink_exp * inv * delta, sinkacc.shape)

        if last:
            for h in range(GROUPS):
                sinksum[h:h + 1, :] = sinkacc[0:1, h * tok:(h + 1) * tok]
            sinksum[GROUPS:, :] = jnp.zeros((8 - GROUPS, tok), F32)
            sinkplanes[z] = sinksum[...]

        for h in range(GROUPS):
            inv_col = jnp.broadcast_to(inv[:, h * tok:(h + 1) * tok], (tok, tok)).T
            for r in (h * tok, lanes + h * tok):
                grhs[r:r + tok, :] = (rhs[slot, r:r + tok, :].astype(F32) * inv_col).astype(BF16)

        if last:
            for p in range(planes):
                @pl.when(p != z)
                def _():
                    sink_to(p).start()

        def grads(c, qgt):
            first = pl.multiple_of(c * chunk, chunk)
            d = (sd[slot, pl.ds(first, chunk), :lanes]
                 * (sd[slot, pl.ds(first, chunk), lanes:] - delta)).astype(BF16)
            ed[pl.ds(first, chunk), :lanes] = d
            acc[pl.ds(start + first, chunk), :] += jnp.dot(
                ed[pl.ds(first, chunk), :], grhs[...], preferred_element_type=F32)
            return qgt + jnp.dot(ktbuf[:, pl.ds(pl.multiple_of(start + first, tok), chunk)], d,
                                 preferred_element_type=F32)

        qgt = lax.fori_loop(0, span // chunk, grads, jnp.zeros((HEAD_DIM, lanes), F32))
        kvgs[b] = acc[rows(b), :].astype(BF16)
        qgt = qgt * (inv * 0.125)
        for pair in range(GROUPS // 2):
            two = jnp.concatenate(
                [qgt[:, (2 * pair + i) * tok:(2 * pair + i + 1) * tok] for i in (0, 1)], 0)
            qgs[b, :, pair * tok:(pair + 1) * tok] = two.T.astype(BF16)

        @pl.when(k > 0)
        def _():
            qg_back(k).start()

        @pl.when((k > 1) & (z > 0))
        def _():
            kg_prev(k).start()
        return ahead

    prepare(0, 0)
    top = lax.fori_loop(0, span // chunk, lambda c, t: scores(c, 0, 0, t), floor)
    top = lax.fori_loop(0, side - 1, lambda k, t: step(k, t, False), top)
    step(side - 1, top, True)

    for j in (l, flip(l, 1)):
        kvgs[j] = acc[rows(j), :].astype(BF16)
    for j in range(side, 2 * side):
        kvgs[j] = acc[j * tok:(j + 1) * tok, :].astype(BF16)
    oq_ref[:, head_cols(l)] = qgs[l]
    kvin[l] = kvgs[side + l]

    def kg_own(k):
        d = flip(l, k)
        return remote(kvgs.at[side + d], kvin.at[l], s_kg.at[side + k], r_kg.at[side + l], base + d)

    @pl.when(z > 0)
    def _():
        kg_prev(0).start()
        kg_prev(1).start()

    for k in range(1, side):
        kg_own(k).start()

    for p in range(planes):
        @pl.when(p != z)
        def _():
            remote(sinksum, sinkplanes.at[p], s_sa.at[p], r_sa.at[p], other).wait_recv()

    sinkall[l] = jnp.sum(sinkplanes[...], 0)

    def sink_side(k):
        return remote(sinkall.at[l], sinkall.at[l], s_sb.at[k], r_sb.at[l], base + flip(l, k))

    for k in range(1, side):
        sink_side(k).start()

    for k in range(1, side):
        j = flip(l, k)
        remote(kvgs.at[0], kvin.at[j], s_kg.at[0], r_kg.at[side + j], other).wait_recv()

    @pl.when(z < planes - 1)
    def _():
        for k in range(side):
            remote(kvgs.at[0], kvnx.at[k], s_kg.at[0], r_kg.at[k], other).wait_recv()

    for pair in range(side // 2):
        two = [kvin[2 * pair + i].astype(F32) + kvnx[2 * pair + i].astype(F32) for i in (0, 1)]
        part = slice(pair * 2 * HEAD_DIM, (pair + 1) * 2 * HEAD_DIM)
        ok_ref[:, part] = jnp.concatenate([t[:, :HEAD_DIM] for t in two], 1).astype(BF16)
        ov_ref[:, part] = jnp.concatenate([t[:, HEAD_DIM:] for t in two], 1).astype(BF16)

    for k in range(1, side):
        j = flip(l, k)
        remote(sinkall.at[j], sinkall.at[j], s_sb.at[0], r_sb.at[j], other).wait_recv()
    place = lax.broadcasted_iota(jnp.int32, sinkall.shape, 2)
    spot = (lax.broadcasted_iota(jnp.int32, sinkall.shape, 0) * GROUPS
            + lax.broadcasted_iota(jnp.int32, sinkall.shape, 1))
    head = lax.broadcasted_iota(jnp.int32, sinkall.shape, 1)
    sums = jnp.sum(sinkall[...], -1, keepdims=True)
    sums = jnp.sum(jnp.where((place == spot) & (head < GROUPS), sums, 0.0), 0)
    os_ref[...] = jnp.sum(sums, 0, keepdims=True)[:, :QUERY_HEADS]

    for k in range(1, side):
        j = flip(l, k)
        remote(qgs.at[0], oq_ref.at[:, head_cols(j)], s_qg.at[0], r_qg.at[j], other).wait_recv()

    @pl.when(z < planes - 1)
    def _():
        for k in range(side):
            for copy in kv_next(k):
                copy.wait_send()

    @pl.when(z > 0)
    def _():
        for k in range(side):
            kg_prev(k).wait_send()

    for p in range(planes):
        @pl.when(p != z)
        def _():
            sink_to(p).wait_send()

    for k in range(1, side):
        for copy in kv_own(k) + qg_to(k) + (qg_back(k), kg_own(k), sink_side(k)):
            copy.wait_send()


def turn(l, k, side):
    pairs = side // 2
    pair = k // 2
    later = (pair + pairs - 1) // pairs
    own = l + (k % 2) * (1 - 2 * (l % 2))
    other = pair - 1 + (pair - 1 - l // 2 + pairs) // pairs
    return (1 - later) * own + later * (2 * other + k % 2)


def write_out(*refs):
    copies = [pltpu.make_async_copy(refs[i], refs[4 + i], refs[8].at[i]) for i in range(4)]
    for copy in copies:
        copy.start()
    for copy in copies:
        copy.wait()


def per_device(queries, key_heads, value_heads, out_grad, segment, sink_logits):
    tok = queries.shape[0]
    planes = lax.axis_size("ctx") // KV_HEADS
    side = KV_HEADS
    cols = GROUPS * HEAD_DIM
    lanes = GROUPS * tok
    span = WINDOW + tok
    chunk = span // 3
    wide = 2 * HEAD_DIM
    vmem = pl.BlockSpec(memory_space=pltpu.VMEM)
    dma = pltpu.SemaphoreType.DMA
    hbm = pl.BlockSpec(memory_space=pltpu.HBM)
    scratch = [
        pltpu.SMEM((QUERY_HEADS,), F32),
        pltpu.VMEM(key_heads.shape, BF16),
        pltpu.VMEM(key_heads.shape, BF16),
        pltpu.VMEM((1, tok), jnp.int32),
        dma((6,)),
        pltpu.VMEM((side, tok, wide), BF16),
        pltpu.VMEM((8, tok), F32),
        pltpu.VMEM((2 * WINDOW, wide), BF16),
        pltpu.VMEM((2 * side, 8, tok), F32),
        pltpu.VMEM((side, tok, cols), BF16),
        pltpu.VMEM((side, tok, cols), BF16),
        pltpu.VMEM((HEAD_DIM, 2 * WINDOW), BF16),
        pltpu.VMEM((2 * WINDOW, tok), F32),
        pltpu.VMEM((2, 2 * lanes, wide), BF16),
        pltpu.VMEM((2 * lanes, wide), BF16),
        pltpu.VMEM((2, span, 2 * lanes), F32),
        pltpu.VMEM((span, 2 * lanes), BF16),
        pltpu.VMEM((2 * WINDOW, wide), F32),
        pltpu.VMEM((side, tok, cols), BF16),
        pltpu.VMEM((2 * side, tok, wide), BF16),
        pltpu.VMEM((side, tok, wide), BF16),
        pltpu.VMEM((side, tok, wide), BF16),
        pltpu.VMEM((8, lanes), F32),
        pltpu.VMEM((planes, 8, tok), F32),
        pltpu.VMEM((8, tok), F32),
        pltpu.VMEM((side, 8, tok), F32),
        dma((2 * side,)), dma((2 * side,)), dma((2 * side,)), dma((2 * side,)),
        dma((side,)), dma((side,)), dma((side,)), dma((side,)),
        dma((side,)), dma((side,)), dma((2 * side,)), dma((2 * side,)),
        dma((planes,)), dma((planes,)), dma((side,)), dma((side,)),
    ]
    shapes = (
        jax.ShapeDtypeStruct(queries.shape, BF16),
        jax.ShapeDtypeStruct(key_heads.shape, BF16),
        jax.ShapeDtypeStruct(value_heads.shape, BF16),
        jax.ShapeDtypeStruct((1, QUERY_HEADS), F32),
    )
    results = pl.pallas_call(
        functools.partial(kernel, planes, chunk),
        out_shape=shapes,
        in_specs=[hbm] * 6,
        out_specs=(vmem,) * 4,
        scratch_shapes=scratch,
        compiler_params=pltpu.CompilerParams(
            collective_id=0, has_side_effects=True, vmem_limit_bytes=48 * 1024 * 1024),
    )(*[pltpu.with_memory_space_constraint(a, pltpu.HBM) for a in (sink_logits, queries, key_heads, value_heads, out_grad, segment.reshape(1, tok))])
    query_grad, key_grad, value_grad, sink = pl.pallas_call(
        write_out,
        out_shape=shapes,
        in_specs=[vmem] * 4,
        out_specs=(hbm,) * 4,
        scratch_shapes=[dma((4,))],
        compiler_params=pltpu.CompilerParams(vmem_limit_bytes=1024 * 1024),
    )(*results)
    return query_grad, key_grad, value_grad, sink.reshape(-1)


def solution(mesh):
    return jax.shard_map(
        per_device,
        mesh=mesh,
        in_specs=(P("ctx", None), P("ctx", None), P("ctx", None), P("ctx", None), P("ctx"), P()),
        out_specs=(P("ctx", None), P("ctx", None), P("ctx", None), P()),
        check_vma=False,
    )
```
